32 devices in a mesh: cols: 4 (over y, core), cells: 8 (over z, x).
Axes of the slice: x: 2, y: 2, z: 4, core: 2. Of those that a mesh axis runs over, the one named last changes fastest.
Arguments:
- slab_cols: float32 [256, 65536], P('cols', 'cells'), may hold values from -6 to 6
- observed_cov: float32 [2, 16, 65536], P(None, 'cols', 'cells'), may hold values from -1 to 30, as said below
- observed_cells: int32 [2, 16], replicated, may hold values from 0 to 65535, as said below
- noise_variance: float32 [2, 16], replicated, may hold values from 1 to 8
- wind_across: float32 [128, 512], P('cells'), may hold values from 0.25 to 0.5
- wind_along: float32 [128, 512], P('cells'), may hold values from -0.3 to 0.3
- diffusion: float32 [128, 512], P('cells'), may hold values from 0.125 to 0.25
Outputs:
- forecast: float32 [256, 65536], P('cols', 'cells')
The draws below stay inside these ranges and needn't reach their ends.
Inputs may be any that keep to these rules, and one draw needn't show every extreme that they name: `observed_cells`: the 32 observed cells are all different, so the two updates observe different cells. observed_cov[u, k, observed_cells[u, k]] lies between 20 and 30; every other entry lies between -1 and 1.
All inputs are finite; a program needn't handle non-finite values.
Results may differ from the reference program's by a relative error of at most 0.00012.
Values sent between devices are 32-bit elements; how exact they have to be, the bound alone decides.
No kernel may reach another device: no remote copies, remote signals or barrier semaphores. Data moves between devices by JAX's collectives and lax.ppermute only.
A program may use at most 64 MiB of HBM per device.

```python
import math
import jax
import jax.numpy as jnp
from jax import lax

GY = 512
K = 16
SECTIONS = 8
SLAB = 256
GX = 128
NCELL = 65536


def chosen_cells(key):
    shuffled = jax.random.permutation(jax.random.fold_in(key, 7), NCELL)
    return shuffled[:2 * K].reshape(2, K).astype(jnp.int32)


def draw_observed_cells(key, part):
    return chosen_cells(key)


def draw_observed_cov(key, part):
    cells = chosen_cells(key)
    all_cells = cells.reshape(2 * K)
    entries = jax.random.uniform(jax.random.fold_in(key, 11), (2, K, NCELL), jnp.float32, -1.0, 1.0)
    coherent = jax.random.uniform(jax.random.fold_in(key, 19), (2, K, 2 * K), jnp.float32, 0.6, 1.0)
    entries = entries.at[:, :, all_cells].set(coherent)
    variance = jax.random.uniform(jax.random.fold_in(key, 13), (2, K), jnp.float32, 20.0, 30.0)
    update_ids = jnp.arange(2)[:, None]
    row_ids = jnp.arange(K)[None, :]
    return entries.at[update_ids, row_ids, cells].set(variance)


def draw_slab_cols(key, part):
    all_cells = chosen_cells(key).reshape(2 * K)
    entries = jax.random.truncated_normal(jax.random.fold_in(key, 21), -6.0, 6.0, (SLAB, NCELL), jnp.float32)
    picked = jax.random.uniform(jax.random.fold_in(key, 23), (SLAB, 2 * K), jnp.float32, 4.0, 6.0)
    return entries.at[:, all_cells].set(picked)


def level_of(rng, extent, shards, low, high):
    loudness = 1.0
    for dim, shards_of in shards:
        draws = jax.random.uniform(jax.random.fold_in(jax.random.fold_in(rng, 6), dim), (shards_of,), jnp.float32, low / len(shards), high / len(shards))
        loudness = loudness * jnp.repeat(jnp.exp(draws), extent[dim] // shards_of).reshape((-1,) + (1,) * (len(extent) - 1 - dim))
    return loudness


def setup_inputs(seed: int = 0) -> dict:
    streams_of = jax.random.split(jax.random.key(seed), 8)
    slab_cols = draw_slab_cols(jax.random.fold_in(streams_of[7], 71), 0)
    observed_cov = draw_observed_cov(jax.random.fold_in(streams_of[7], 71), 0)
    observed_cells = draw_observed_cells(jax.random.fold_in(streams_of[7], 71), 0)
    noise_variance = jnp.clip(jnp.exp(jax.random.uniform(streams_of[3], (2, K), jnp.float32, math.log(1.0), math.log(8.0))), 1.0, 8.0)
    wind_across = jnp.clip(0.25 + 0.25 * jax.random.uniform(streams_of[4], (GX, GY), jnp.float32) ** level_of(streams_of[4], (GX, GY), ((0, 8),), -0.2, 0.2), 0.25, 0.5)
    wind_along = jnp.clip(jax.random.uniform(streams_of[5], (GX, GY), jnp.float32, -0.3, 0.3) * level_of(streams_of[5], (GX, GY), ((0, 8),), -0.4, 0.0), -0.3, 0.3)
    diffusion = jnp.clip(0.125 + 0.125 * jax.random.uniform(streams_of[6], (GX, GY), jnp.float32) ** level_of(streams_of[6], (GX, GY), ((0, 8),), -0.2, 0.2), 0.125, 0.25)
    return {"slab_cols": slab_cols, "observed_cov": observed_cov, "observed_cells": observed_cells, "noise_variance": noise_variance, "wind_across": wind_across, "wind_along": wind_along, "diffusion": diffusion}


def invert_small(matrix):
    dimension = matrix.shape[0]
    joined = jnp.concatenate([matrix, jnp.eye(dimension, dtype=matrix.dtype)], axis=1)
    for column in range(dimension):
        scaled = joined[column] / joined[column, column]
        joined = joined - joined[:, column:column + 1] * scaled[None, :]
        joined = joined.at[column].set(scaled)
    return joined[:, dimension:]


def symmetric(block):
    return 0.5 * (block + block.T)


def product(left, right):
    return jnp.dot(left, right, precision=lax.Precision.HIGHEST, preferred_element_type=jnp.float32)


def advance(field, across, along, spread):
    above_row = jnp.roll(field, -1, axis=1)
    below_row = jnp.roll(field, 1, axis=1)
    east_cell = jnp.roll(field, -1, axis=2)
    west_cell = jnp.roll(field, 1, axis=2)
    return field - 0.5 * across * (above_row - below_row) - 0.5 * along * (east_cell - west_cell) + spread * (above_row + below_row + east_cell + west_cell - 4.0 * field)


def reference(slab_cols, observed_cov, observed_cells, noise_variance, wind_across, wind_along, diffusion):
    first_cells = observed_cells[0]
    second_cells = observed_cells[1]
    first_cov = observed_cov[0]
    second_cov = observed_cov[1]
    first_block = first_cov[:, first_cells]
    cross_block = first_cov[:, second_cells]
    second_block = second_cov[:, second_cells]
    first_matrix = symmetric(first_block) + jnp.diag(noise_variance[0])
    first_inverse = invert_small(first_matrix)
    first_gain = product(first_inverse, first_cov)
    updated = slab_cols - product(slab_cols[:, first_cells], first_gain)
    revised_cov = second_cov - product(cross_block.T, first_gain)
    revised_block = revised_cov[:, second_cells]
    second_matrix = symmetric(revised_block) + jnp.diag(noise_variance[1])
    second_gain = product(invert_small(second_matrix), revised_cov)
    analysis = updated - product(updated[:, second_cells], second_gain)
    field = analysis.reshape(analysis.shape[0], GX, GY)
    for number in range(SECTIONS):
        field = advance(field, wind_across, wind_along, diffusion)
    return field.reshape(analysis.shape[0], NCELL)
```

```python
import jax
import jax.numpy as jnp
from jax import lax
from jax.experimental import pallas as pl
from jax.experimental.pallas import tpu as pltpu
from jax.sharding import PartitionSpec as P

SECTIONS = 8
LANES = 128
SUBLANES = 8
COEFFICIENTS = 5


VMEM = pl.BlockSpec(memory_space=pltpu.VMEM)
SMEM = pl.BlockSpec(memory_space=pltpu.SMEM)


def f32(*shape):
    return jax.ShapeDtypeStruct(shape, jnp.float32)


def cost(flops, moved):
    return pl.CostEstimate(flops=flops, bytes_accessed=moved, transcendentals=0)


def product(left, right, dims=((1,), (0,))):
    return lax.dot_general(
        left,
        right,
        (dims, ((), ())),
        precision=lax.Precision.HIGHEST,
        preferred_element_type=jnp.float32,
    )


def ring(axis, step):
    count = lax.axis_size(axis)
    return [(i, (i + step) % count) for i in range(count)]


def swap(value, axis, bit):
    count = lax.axis_size(axis)
    return lax.ppermute(value, axis, [(i, i ^ bit) for i in range(count)])


def bits_of(axis):
    count = lax.axis_size(axis)
    bits = []
    bit = 1
    while bit < count:
        bits.append(bit)
        bit *= 2
    assert bit == count
    return bits


def pack(cov_ref, across_ref, along_ref, spread_ref, own_ref, up_ref, down_ref):
    updates, held, cells = cov_ref.shape
    rows, width = across_ref.shape
    edge = SECTIONS * width
    if own_ref.shape[0] > updates * held:
        own_ref[...] = jnp.zeros_like(own_ref)
    for update in range(updates):
        own_ref[update * held : (update + 1) * held, :] = cov_ref[update]
    for out_ref, start in ((up_ref, rows - SECTIONS), (down_ref, 0)):
        if out_ref.shape[0] > SECTIONS:
            out_ref[...] = jnp.zeros_like(out_ref)
        out_ref[:, :edge] = own_ref[:, start * width : start * width + edge]
        for number, wind_ref in enumerate((across_ref, along_ref, spread_ref)):
            at = edge + number * width
            out_ref[:SECTIONS, at : at + width] = wind_ref[start : start + SECTIONS, :]


def select(cells_ref, slab_ref, cov_ref, picks_ref, blocks_ref, *halo_refs):
    updates, count = cells_ref.shape
    fields, cells = slab_ref.shape
    offset = lax.axis_index("cells") * cells
    picks_ref[...] = jnp.zeros_like(picks_ref)
    blocks_ref[...] = jnp.zeros_like(blocks_ref)
    mine = lax.axis_index("cols")

    def pick(number, carry):
        position = cells_ref[number // count, number % count] - offset

        @pl.when((position >= 0) & (position < cells))
        def _():
            lane = position % LANES
            start = pl.multiple_of(position - lane, LANES)
            shift = (number + LANES - lane) % LANES
            for out, source in ((picks_ref, slab_ref), (blocks_ref.at[mine], cov_ref)):
                tile = pltpu.roll(source[:, pl.ds(start, LANES)], shift, 1)
                at = lax.broadcasted_iota(jnp.int32, tile.shape, 1)
                out[...] = jnp.where(at == number, tile, out[...])

        return carry

    lax.fori_loop(0, updates * count, pick, 0)
    chunks = len(halo_refs) // 2
    part = fields // chunks
    for chunk in range(chunks):
        here = pl.ds(chunk * part, part)
        edge = halo_refs[2 * chunk].shape[1]
        halo_refs[2 * chunk][...] = slab_ref[here, cells - edge :]
        halo_refs[2 * chunk + 1][...] = slab_ref[here, :edge]


def invert_small(matrix):
    size = matrix.shape[0]
    row = lax.broadcasted_iota(jnp.int32, (size, size), 0)
    col = lax.broadcasted_iota(jnp.int32, (size, size), 1)
    joined = jnp.concatenate([matrix, jnp.where(row == col, 1.0, 0.0)], axis=1)
    row = lax.broadcasted_iota(jnp.int32, joined.shape, 0)
    for column in range(size):
        scaled = joined[column : column + 1, :] / joined[column : column + 1, column : column + 1]
        reduced = joined - joined[:, column : column + 1] * scaled
        joined = jnp.where(row == column, jnp.broadcast_to(scaled, joined.shape), reduced)
    return joined[:, size:]


def coefficients(order, held, picks_ref, blocks_ref, noise_ref, out_ref, joined_ref):
    shards, padded, _ = blocks_ref.shape
    updates, count = noise_ref.shape
    for shard in range(shards):
        for update in range(updates):
            at = update * count + shard * held
            joined_ref[at : at + held, :] = blocks_ref[shard, update * held : (update + 1) * held, :]
    row = lax.broadcasted_iota(jnp.int32, (count, count), 0)
    col = lax.broadcasted_iota(jnp.int32, (count, count), 1)
    eye = jnp.where(row == col, 1.0, 0.0)

    def second(value):
        return pltpu.roll(value, LANES - count, 1)[:, :count]

    def regular(block, update):
        turned = product(block, eye, ((0,), (0,)))
        noise = jnp.broadcast_to(noise_ref[update : update + 1, :], (count, count))
        return 0.5 * (block + turned) + eye * noise

    first_rows = joined_ref[:count, :]
    cross = second(first_rows)
    inverse = invert_small(regular(first_rows[:, :count], 0))
    cross_gain = product(inverse, cross)
    revised = second(joined_ref[count:, :]) - product(cross, cross_gain, ((0,), (0,)))
    second_inverse = invert_small(regular(revised, 1))
    picks = picks_ref[...]
    first_picks = picks[:, :count]
    second_picks = second(picks) - product(first_picks, cross_gain)
    later = product(second_picks, second_inverse)
    earlier = product(first_picks - product(later, cross, ((1,), (1,))), inverse)
    mine = lax.axis_index("cols")
    total = jnp.zeros(out_ref.shape, jnp.float32)
    source = lax.broadcasted_iota(jnp.int32, (count, out_ref.shape[1]), 0)
    target = lax.broadcasted_iota(jnp.int32, (count, out_ref.shape[1]), 1)
    for update, value in enumerate((earlier, later)):
        place = jnp.full(source.shape, -1, jnp.int32)
        for slot, other in enumerate(order):
            shard = mine ^ other
            for index in range(held):
                hit = source == shard * held + index
                place = jnp.where(hit, slot * padded + update * held + index, place)
        total = total + product(value, jnp.where(target == place, 1.0, 0.0))
    out_ref[...] = total


def correction(*refs):
    out_ref = refs[-1]
    coefficient_ref = refs[0]
    part_refs = refs[1:-1]
    padded = part_refs[0].shape[0]
    width = 512
    for start in range(0, out_ref.shape[1], width):
        here = slice(start, start + width)
        stacked = jnp.concatenate([part[:, here] for part in part_refs], axis=0)
        out_ref[:, here] = -product(coefficient_ref[...], stacked)


def sections(buffer_ref, weight_ref, finish):
    total, fields, width = buffer_ref.shape

    def weight(number, row):
        line = weight_ref[number, pl.ds(row, 1), :]
        return jnp.broadcast_to(line, (fields, width))

    for number in range(1, SECTIONS + 1):

        def step(row, carry, last=number == SECTIONS):
            below, center = carry
            above = buffer_ref[row + 1]
            east = pltpu.roll(center, width - 1, 1)
            west = pltpu.roll(center, 1, 1)
            value = (
                weight(0, row) * center
                + weight(1, row) * above
                + weight(2, row) * below
                + weight(3, row) * east
                + weight(4, row) * west
            )
            if last:
                finish(row - SECTIONS, value)
            else:
                buffer_ref[row] = value
            return center, above

        lax.fori_loop(
            number,
            total - number,
            step,
            (buffer_ref[number - 1], buffer_ref[number]),
        )


def fill(buffer_ref, low_ref, own_ref, high_ref):
    total, _, width = buffer_ref.shape
    rows = total - 2 * SECTIONS
    for row in range(SECTIONS):
        here = slice(row * width, (row + 1) * width)
        buffer_ref[row] = low_ref[:, here]
        buffer_ref[rows + SECTIONS + row] = high_ref[:, here]
    for row in range(rows):
        buffer_ref[SECTIONS + row] = own_ref[:, row * width : (row + 1) * width]


def forecast_cov(
    own_ref, low_ref, high_ref, across_ref, along_ref, spread_ref, out_ref, weight_ref, buffer_ref
):
    rows, width = across_ref.shape
    edge = SECTIONS * width

    def whole(number, wind_ref):
        at = edge + number * width
        low = low_ref[:SECTIONS, at : at + width]
        high = high_ref[:SECTIONS, at : at + width]
        return jnp.concatenate([low, wind_ref[...], high], axis=0)

    across = 0.5 * whole(0, across_ref)
    along = 0.5 * whole(1, along_ref)
    spread = whole(2, spread_ref)
    weight_ref[0] = 1.0 - 4.0 * spread
    weight_ref[1] = spread - across
    weight_ref[2] = spread + across
    weight_ref[3] = spread - along
    weight_ref[4] = spread + along
    fill(buffer_ref, low_ref, own_ref, high_ref)

    def finish(row, value):
        out_ref[:, pl.ds(pl.multiple_of(row * width, width), width)] = value

    sections(buffer_ref, weight_ref, finish)


def forecast_slab(slab_ref, low_ref, high_ref, weight_ref, held_ref, out_ref, buffer_ref):
    width = buffer_ref.shape[2]
    fill(buffer_ref, low_ref, slab_ref, high_ref)

    def finish(row, value):
        here = pl.ds(pl.multiple_of(row * width, width), width)
        out_ref[:, here] = held_ref[:, here] + value

    sections(buffer_ref, weight_ref, finish)


def local(
    slab_cols, observed_cov, observed_cells, noise_variance, wind_across, wind_along, diffusion
):
    fields, cells = slab_cols.shape
    updates, held, _ = observed_cov.shape
    rows, width = wind_across.shape
    edge = SECTIONS * width
    total_rows = rows + 2 * SECTIONS
    padded = -(-updates * held // SUBLANES) * SUBLANES
    shards = lax.axis_size("cols")
    part = 2 * SUBLANES
    chunks = fields // part
    winds = (wind_across, wind_along, diffusion)

    cov_own, cov_up, cov_down = pl.pallas_call(
        pack,
        out_shape=(f32(padded, cells), f32(padded, edge + 3 * width), f32(padded, edge + 3 * width)),
        in_specs=[VMEM] * 4,
        out_specs=(VMEM,) * 3,
        cost_estimate=cost(0, 8 * padded * cells),
        name="pack",
    )(observed_cov, *winds)
    cov_low = lax.ppermute(cov_up, "cells", ring("cells", 1))
    cov_high = lax.ppermute(cov_down, "cells", ring("cells", -1))

    picks, blocks, *halos = pl.pallas_call(
        select,
        out_shape=(f32(fields, LANES), f32(shards, padded, LANES)) + (f32(part, edge),) * (2 * chunks),
        in_specs=[SMEM, VMEM, VMEM],
        out_specs=(VMEM,) * (2 + 2 * chunks),
        cost_estimate=cost(0, 8 * fields * cells),
        name="select",
    )(observed_cells, slab_cols, cov_own)
    small = jnp.concatenate([picks, blocks.reshape(shards * padded, LANES)])
    bits = bits_of("cells")
    small = small + swap(small, "cells", bits[0])
    arrived = []
    for chunk in range(chunks):
        low = lax.ppermute(halos[2 * chunk], "cells", ring("cells", 1))
        high = lax.ppermute(halos[2 * chunk + 1], "cells", ring("cells", -1))
        arrived.append((low, high))
    for bit in bits[1:]:
        small = small + swap(small, "cells", bit)
    picks = small[:fields]
    blocks = small[fields:]
    for bit in bits_of("cols"):
        blocks = blocks + swap(blocks, "cols", bit)

    cov_after, weights = pl.pallas_call(
        forecast_cov,
        out_shape=(f32(padded, cells), f32(COEFFICIENTS, total_rows, width)),
        in_specs=[VMEM] * 6,
        out_specs=(VMEM,) * 2,
        scratch_shapes=[pltpu.VMEM((total_rows, padded, width), jnp.float32)],
        cost_estimate=cost(80 * padded * cells, 16 * padded * cells),
        name="forecast_cov",
    )(cov_own, cov_low, cov_high, *winds)
    order = [0]
    parts = [cov_after]
    for bit in reversed(bits_of("cols")):
        order = order + [other ^ bit for other in order]
        parts = parts + [swap(value, "cols", bit) for value in parts]

    def build(*refs):
        coefficients(order, held, *refs)

    gains = pl.pallas_call(
        build,
        out_shape=f32(fields, shards * padded),
        in_specs=[VMEM] * 3,
        out_specs=VMEM,
        scratch_shapes=[pltpu.VMEM((updates * noise_variance.shape[1], LANES), jnp.float32)],
        cost_estimate=cost(10**7, 10**6),
        name="coefficients",
    )(picks, blocks.reshape(shards, padded, LANES), noise_variance)
    result = pl.pallas_call(
        correction,
        out_shape=f32(fields, cells),
        in_specs=[VMEM] * (1 + len(parts)),
        out_specs=VMEM,
        cost_estimate=cost(12 * fields * shards * padded * cells, 4 * fields * cells),
        name="correction",
    )(gains, *parts)
    for chunk, (low, high) in enumerate(arrived):
        whole = pl.BlockSpec((part, cells), lambda step, chunk=chunk: (chunk, 0))
        side = pl.BlockSpec((part, edge), lambda step: (0, 0))
        weight = pl.BlockSpec((COEFFICIENTS, total_rows, width), lambda step: (0, 0, 0))
        result = pl.pallas_call(
            forecast_slab,
            out_shape=f32(fields, cells),
            grid=(1,),
            in_specs=[whole, side, side, weight, whole],
            out_specs=whole,
            scratch_shapes=[pltpu.VMEM((total_rows, part, width), jnp.float32)],
            input_output_aliases={4: 0},
            cost_estimate=cost(120 * part * cells, 16 * part * cells),
            name=f"forecast_slab_{chunk}",
        )(slab_cols, low, high, weights, result)
    return result


def solution(mesh):
    return jax.shard_map(
        local,
        mesh=mesh,
        in_specs=(
            P("cols", "cells"),
            P(None, "cols", "cells"),
            P(),
            P(),
            P("cells", None),
            P("cells", None),
            P("cells", None),
        ),
        out_specs=P("cols", "cells"),
        check_vma=False,
    )
```

```python
import jax
import jax.numpy as jnp
from jax import lax
from jax.experimental import pallas as pl
from jax.experimental.pallas import tpu as pltpu
from jax.sharding import PartitionSpec as P

SECTIONS = 8
LANES = 128
SUBLANES = 8
COEFFICIENTS = 5


VMEM = pl.BlockSpec(memory_space=pltpu.VMEM)
SMEM = pl.BlockSpec(memory_space=pltpu.SMEM)


def f32(*shape):
    return jax.ShapeDtypeStruct(shape, jnp.float32)


def cost(flops, moved):
    return pl.CostEstimate(flops=flops, bytes_accessed=moved, transcendentals=0)


LIMIT = pltpu.CompilerParams(vmem_limit_bytes=16 * 1024 * 1024)


def product(left, right, dims=((1,), (0,))):
    return lax.dot_general(
        left,
        right,
        (dims, ((), ())),
        precision=lax.Precision.HIGHEST,
        preferred_element_type=jnp.float32,
    )


def ring(axis, step):
    count = lax.axis_size(axis)
    return [(i, (i + step) % count) for i in range(count)]


def swap(value, axis, bit):
    count = lax.axis_size(axis)
    return lax.ppermute(value, axis, [(i, i ^ bit) for i in range(count)])


def bits_of(axis):
    count = lax.axis_size(axis)
    bits = []
    bit = 1
    while bit < count:
        bits.append(bit)
        bit *= 2
    assert bit == count
    return bits


def pack(cov_ref, across_ref, along_ref, spread_ref, own_ref, up_ref, down_ref):
    updates, held, cells = cov_ref.shape
    rows, width = across_ref.shape
    edge = SECTIONS * width
    if own_ref.shape[0] > updates * held:
        own_ref[...] = jnp.zeros_like(own_ref)
    for update in range(updates):
        own_ref[update * held : (update + 1) * held, :] = cov_ref[update]
    for out_ref, start in ((up_ref, rows - SECTIONS), (down_ref, 0)):
        if out_ref.shape[0] > SECTIONS:
            out_ref[...] = jnp.zeros_like(out_ref)
        out_ref[:, :edge] = own_ref[:, start * width : start * width + edge]
        for number, wind_ref in enumerate((across_ref, along_ref, spread_ref)):
            at = edge + number * width
            out_ref[:SECTIONS, at : at + width] = wind_ref[start : start + SECTIONS, :]


def select(cells_ref, slab_ref, cov_ref, picks_ref, blocks_ref, *halo_refs):
    updates, count = cells_ref.shape
    fields, cells = slab_ref.shape
    offset = lax.axis_index("cells") * cells
    picks_ref[...] = jnp.zeros_like(picks_ref)
    blocks_ref[...] = jnp.zeros_like(blocks_ref)
    mine = lax.axis_index("cols")

    def pick(number, carry):
        position = cells_ref[number // count, number % count] - offset

        @pl.when((position >= 0) & (position < cells))
        def _():
            lane = position % LANES
            start = pl.multiple_of(position - lane, LANES)
            shift = (number + LANES - lane) % LANES
            for out, source in ((picks_ref, slab_ref), (blocks_ref.at[mine], cov_ref)):
                tile = pltpu.roll(source[:, pl.ds(start, LANES)], shift, 1)
                at = lax.broadcasted_iota(jnp.int32, tile.shape, 1)
                out[...] = jnp.where(at == number, tile, out[...])

        return carry

    lax.fori_loop(0, updates * count, pick, 0)
    chunks = len(halo_refs) // 2
    part = fields // chunks
    for chunk in range(chunks):
        here = pl.ds(chunk * part, part)
        edge = halo_refs[2 * chunk].shape[1]
        halo_refs[2 * chunk][...] = slab_ref[here, cells - edge :]
        halo_refs[2 * chunk + 1][...] = slab_ref[here, :edge]


def invert_small(matrix):
    size = matrix.shape[0]
    row = lax.broadcasted_iota(jnp.int32, (size, size), 0)
    col = lax.broadcasted_iota(jnp.int32, (size, size), 1)
    joined = jnp.concatenate([matrix, jnp.where(row == col, 1.0, 0.0)], axis=1)
    row = lax.broadcasted_iota(jnp.int32, joined.shape, 0)
    for column in range(size):
        scaled = joined[column : column + 1, :] / joined[column : column + 1, column : column + 1]
        reduced = joined - joined[:, column : column + 1] * scaled
        joined = jnp.where(row == column, jnp.broadcast_to(scaled, joined.shape), reduced)
    return joined[:, size:]


def coefficients(order, held, picks_ref, blocks_ref, noise_ref, out_ref, joined_ref):
    shards, padded, _ = blocks_ref.shape
    updates, count = noise_ref.shape
    for shard in range(shards):
        for update in range(updates):
            at = update * count + shard * held
            joined_ref[at : at + held, :] = blocks_ref[shard, update * held : (update + 1) * held, :]
    row = lax.broadcasted_iota(jnp.int32, (count, count), 0)
    col = lax.broadcasted_iota(jnp.int32, (count, count), 1)
    eye = jnp.where(row == col, 1.0, 0.0)

    def second(value):
        return pltpu.roll(value, LANES - count, 1)[:, :count]

    def regular(block, update):
        turned = product(block, eye, ((0,), (0,)))
        noise = jnp.broadcast_to(noise_ref[update : update + 1, :], (count, count))
        return 0.5 * (block + turned) + eye * noise

    first_rows = joined_ref[:count, :]
    cross = second(first_rows)
    inverse = invert_small(regular(first_rows[:, :count], 0))
    cross_gain = product(inverse, cross)
    revised = second(joined_ref[count:, :]) - product(cross, cross_gain, ((0,), (0,)))
    second_inverse = invert_small(regular(revised, 1))
    picks = picks_ref[...]
    first_picks = picks[:, :count]
    second_picks = second(picks) - product(first_picks, cross_gain)
    later = product(second_picks, second_inverse)
    earlier = product(first_picks - product(later, cross, ((1,), (1,))), inverse)
    mine = lax.axis_index("cols")
    total = jnp.zeros(out_ref.shape, jnp.float32)
    source = lax.broadcasted_iota(jnp.int32, (count, out_ref.shape[1]), 0)
    target = lax.broadcasted_iota(jnp.int32, (count, out_ref.shape[1]), 1)
    for update, value in enumerate((earlier, later)):
        place = jnp.full(source.shape, -1, jnp.int32)
        for slot, other in enumerate(order):
            shard = mine ^ other
            for index in range(held):
                hit = source == shard * held + index
                place = jnp.where(hit, slot * padded + update * held + index, place)
        total = total + product(value, jnp.where(target == place, 1.0, 0.0))
    out_ref[...] = total


def split(value):
    pieces = []
    for _ in range(3):
        piece = value.astype(jnp.bfloat16)
        pieces.append(piece)
        value = value - piece.astype(jnp.float32)
    return pieces


TERMS = ((0, 0), (0, 1), (1, 0), (0, 2), (2, 0), (1, 1))


def correction(*refs):
    out_ref = refs[-1]
    part_refs = refs[1:-1]
    pieces = split(refs[0][...])
    left = jnp.concatenate([pieces[one] for one, _ in TERMS], axis=1)
    width = 512
    for start in range(0, out_ref.shape[1], width):
        here = slice(start, start + width)
        pieces = split(jnp.concatenate([part[:, here] for part in part_refs], axis=0))
        right = jnp.concatenate([pieces[other] for _, other in TERMS], axis=0)
        out_ref[:, here] = -jnp.dot(left, right, preferred_element_type=jnp.float32)


def sections(buffer_ref, weight_ref, finish):
    total, fields, width = buffer_ref.shape

    def weight(number, row):
        line = weight_ref[number, row : row + 1, :]
        return jnp.broadcast_to(line, (fields, width))

    for number in range(1, SECTIONS + 1):

        def step(row, carry, last=number == SECTIONS):
            below, center = carry
            above = buffer_ref[row + 1]
            east = pltpu.roll(center, width - 1, 1)
            west = pltpu.roll(center, 1, 1)
            value = (
                weight(0, row) * center
                + weight(1, row) * above
                + weight(2, row) * below
                + weight(3, row) * east
                + weight(4, row) * west
            )
            if last:
                finish(row - SECTIONS, value)
            else:
                buffer_ref[row] = value
            return center, above

        carry = (buffer_ref[number - 1], buffer_ref[number])
        for row in range(number, total - number):
            carry = step(row, carry)


def fill(buffer_ref, low_ref, own_ref, high_ref):
    total, _, width = buffer_ref.shape
    rows = total - 2 * SECTIONS
    for row in range(SECTIONS):
        here = slice(row * width, (row + 1) * width)
        buffer_ref[row] = low_ref[:, here]
        buffer_ref[rows + SECTIONS + row] = high_ref[:, here]
    for row in range(rows):
        buffer_ref[SECTIONS + row] = own_ref[:, row * width : (row + 1) * width]


def forecast_cov(
    own_ref, low_ref, high_ref, across_ref, along_ref, spread_ref, out_ref, weight_ref, buffer_ref
):
    rows, width = across_ref.shape
    edge = SECTIONS * width

    def whole(number, wind_ref):
        at = edge + number * width
        low = low_ref[:SECTIONS, at : at + width]
        high = high_ref[:SECTIONS, at : at + width]
        return jnp.concatenate([low, wind_ref[...], high], axis=0)

    across = 0.5 * whole(0, across_ref)
    along = 0.5 * whole(1, along_ref)
    spread = whole(2, spread_ref)
    weight_ref[0] = 1.0 - 4.0 * spread
    weight_ref[1] = spread - across
    weight_ref[2] = spread + across
    weight_ref[3] = spread - along
    weight_ref[4] = spread + along
    fill(buffer_ref, low_ref, own_ref, high_ref)

    def finish(row, value):
        out_ref[:, pl.ds(row * width, width)] = value

    sections(buffer_ref, weight_ref, finish)


def forecast_slab(slab_ref, low_ref, high_ref, weight_ref, held_ref, *refs):
    out_ref, buffer_ref = refs[-2:]
    width = buffer_ref.shape[2]
    fill(buffer_ref, low_ref, slab_ref, high_ref)

    def finish(row, value):
        here = pl.ds(row * width, width)
        out_ref[:, here] = held_ref[:, here] + value

    sections(buffer_ref, weight_ref, finish)


def local(
    slab_cols, observed_cov, observed_cells, noise_variance, wind_across, wind_along, diffusion
):
    fields, cells = slab_cols.shape
    updates, held, _ = observed_cov.shape
    rows, width = wind_across.shape
    edge = SECTIONS * width
    total_rows = rows + 2 * SECTIONS
    padded = -(-updates * held // SUBLANES) * SUBLANES
    shards = lax.axis_size("cols")
    part = 2 * SUBLANES
    chunks = fields // part
    winds = (wind_across, wind_along, diffusion)

    cov_own, cov_up, cov_down = pl.pallas_call(
        pack,
        out_shape=(f32(padded, cells), f32(padded, edge + 3 * width), f32(padded, edge + 3 * width)),
        in_specs=[VMEM] * 4,
        out_specs=(VMEM,) * 3,
        compiler_params=LIMIT,
        cost_estimate=cost(0, 8 * padded * cells),
        name="pack",
    )(observed_cov, *winds)
    cov_low = lax.ppermute(cov_up, "cells", ring("cells", 1))
    cov_high = lax.ppermute(cov_down, "cells", ring("cells", -1))

    picks, blocks, *halos = pl.pallas_call(
        select,
        out_shape=(f32(fields, LANES), f32(shards, padded, LANES)) + (f32(part, edge),) * (2 * chunks),
        in_specs=[SMEM, VMEM, VMEM],
        out_specs=(VMEM,) * (2 + 2 * chunks),
        compiler_params=LIMIT,
        cost_estimate=cost(0, 8 * fields * cells),
        name="select",
    )(observed_cells, slab_cols, cov_own)
    small = jnp.concatenate([picks, blocks.reshape(shards * padded, LANES)])
    bits = bits_of("cells")
    small = small + swap(small, "cells", bits[0])
    arrived = []
    for chunk in range(chunks):
        low = lax.ppermute(halos[2 * chunk], "cells", ring("cells", 1))
        high = lax.ppermute(halos[2 * chunk + 1], "cells", ring("cells", -1))
        arrived.append((low, high))
    for bit in bits[1:]:
        small = small + swap(small, "cells", bit)
    picks = small[:fields]
    blocks = small[fields:]
    for bit in bits_of("cols"):
        blocks = blocks + swap(blocks, "cols", bit)

    cov_after, weights = pl.pallas_call(
        forecast_cov,
        out_shape=(f32(padded, cells), f32(COEFFICIENTS, total_rows, width)),
        in_specs=[VMEM] * 6,
        out_specs=(VMEM,) * 2,
        scratch_shapes=[pltpu.VMEM((total_rows, padded, width), jnp.float32)],
        compiler_params=LIMIT,
        cost_estimate=cost(80 * padded * cells, 16 * padded * cells),
        name="forecast_cov",
    )(cov_own, cov_low, cov_high, *winds)
    order = [0]
    parts = [cov_after]
    for bit in reversed(bits_of("cols")):
        order = order + [other ^ bit for other in order]
        parts = parts + [swap(value, "cols", bit) for value in parts]

    def build(*refs):
        coefficients(order, held, *refs)

    gains = pl.pallas_call(
        build,
        out_shape=f32(fields, shards * padded),
        in_specs=[VMEM] * 3,
        out_specs=VMEM,
        scratch_shapes=[pltpu.VMEM((updates * noise_variance.shape[1], LANES), jnp.float32)],
        compiler_params=LIMIT,
        cost_estimate=cost(10**7, 10**6),
        name="coefficients",
    )(picks, blocks.reshape(shards, padded, LANES), noise_variance)
    result = pl.pallas_call(
        correction,
        out_shape=f32(fields, cells),
        in_specs=[VMEM] * (1 + len(parts)),
        out_specs=VMEM,
        compiler_params=LIMIT,
        cost_estimate=cost(12 * fields * shards * padded * cells, 4 * fields * cells),
        name="correction",
    )(gains, *parts)
    outs = ()
    for chunk, (low, high) in enumerate(arrived):
        whole = pl.BlockSpec((part, cells), lambda step, chunk=chunk: (chunk, 0))
        side = pl.BlockSpec((part, edge), lambda step: (0, 0))
        weight = pl.BlockSpec((COEFFICIENTS, total_rows, width), lambda step: (0, 0, 0))
        outs = (
            pl.pallas_call(
                forecast_slab,
                out_shape=f32(fields, cells),
                grid=(1,),
                in_specs=[whole, side, side, weight, whole]
                + [pl.BlockSpec(memory_space=pl.ANY)] * len(outs),
                out_specs=whole,
                scratch_shapes=[pltpu.VMEM((total_rows, part, width), jnp.float32)],
                input_output_aliases={5: 0} if outs else {},
                compiler_params=LIMIT,
                cost_estimate=cost(120 * part * cells, 16 * part * cells),
                name=f"forecast_slab_{chunk}",
            )(slab_cols, low, high, weights, result, *outs),
        )
    return outs[0]


def solution(mesh):
    return jax.shard_map(
        local,
        mesh=mesh,
        in_specs=(
            P("cols", "cells"),
            P(None, "cols", "cells"),
            P(),
            P(),
            P("cells", None),
            P("cells", None),
            P("cells", None),
        ),
        out_specs=P("cols", "cells"),
        check_vma=False,
    )
```

```python
import functools

import jax
import jax.numpy as jnp
from jax import lax
from jax.experimental import pallas as pl
from jax.experimental.pallas import tpu as pltpu
from jax.sharding import PartitionSpec as P


SECTIONS = 8
LANES = 128
SUBLANES = 8
COEFFICIENTS = 5
CHUNKS = 4
EARLY = 3
STORES = 4


VMEM = pl.BlockSpec(memory_space=pltpu.VMEM)
HBM = pl.BlockSpec(memory_space=pltpu.HBM)


def f32(*shape):
    return jax.ShapeDtypeStruct(shape, jnp.float32)


def cost(flops, moved):
    return pl.CostEstimate(flops=flops, bytes_accessed=moved, transcendentals=0)


def in_hbm(value):
    return pltpu.with_memory_space_constraint(value, pltpu.HBM)


LIMIT = pltpu.CompilerParams(vmem_limit_bytes=16 * 1024 * 1024)


def product(left, right, dims=((1,), (0,))):
    return lax.dot_general(
        left,
        right,
        (dims, ((), ())),
        precision=lax.Precision.HIGHEST,
        preferred_element_type=jnp.float32,
    )


def swap(value, axis, bit):
    count = lax.axis_size(axis)
    return lax.ppermute(value, axis, [(i, i ^ bit) for i in range(count)])


def bits_of(axis):
    count = lax.axis_size(axis)
    bits = []
    bit = 1
    while bit < count:
        bits.append(bit)
        bit *= 2
    assert bit == count
    return bits


def is_even():
    return lax.axis_index("cells") % 2 == 0


def starts_of(rows):
    late = rows - SECTIONS
    return jnp.where(is_even(), late, 0), jnp.where(is_even(), 0, late)


def pack(cov_ref, across_ref, along_ref, spread_ref, own_ref, a_ref, b_ref, cov, sems):
    updates, held, _ = cov_ref.shape
    rows, width = across_ref.shape
    edge = SECTIONS * width
    sends = tuple(zip((a_ref, b_ref), starts_of(rows)))
    copies = [pltpu.make_async_copy(cov_ref, cov, sems.at[0])]
    for side, (send_ref, start) in enumerate(sends):
        here = pl.ds(pl.multiple_of(start, SUBLANES), SECTIONS)
        for number, wind_ref in enumerate((across_ref, along_ref, spread_ref)):
            copies.append(
                pltpu.make_async_copy(
                    wind_ref.at[here, :],
                    send_ref.at[:, pl.ds(edge + number * width, width)],
                    sems.at[1 + 3 * side + number],
                )
            )
    for copy in copies:
        copy.start()
    for copy in copies:
        copy.wait()
    if own_ref.shape[0] > updates * held:
        own_ref[...] = jnp.zeros_like(own_ref)
    for update in range(updates):
        own_ref[update * held : (update + 1) * held, :] = cov[update]
    for send_ref, start in sends:
        send_ref[:, :edge] = own_ref[:, pl.ds(pl.multiple_of(start * width, LANES), edge)]


def select(width, listed_ref, slab_ref, own_ref, held_ref, small_ref, *refs):
    send_refs, (cells_ref, sems) = refs[:-2], refs[-2:]
    updates, count = cells_ref.shape
    fields, cells = slab_ref.shape
    edge = SECTIONS * width
    listed = pltpu.make_async_copy(listed_ref, cells_ref, sems.at[0])
    listed.start()
    pairs = tuple(zip(send_refs[::2], send_refs[1::2]))
    copies = []
    first = 0
    for number, (send_ref, _) in enumerate(pairs):
        here = pl.ds(first, send_ref.shape[0])
        copies.append(
            pltpu.make_async_copy(slab_ref.at[here, :], held_ref.at[here, :], sems.at[1 + number])
        )
        copies[-1].start()
        first += send_ref.shape[0]
    small_ref[...] = jnp.zeros_like(small_ref)
    lanes = [pl.ds(pl.multiple_of(start * width, LANES), edge) for start in starts_of(cells // width)]
    first = 0
    for copy, pair in zip(copies, pairs):
        copy.wait()
        part = pair[0].shape[0]
        for side in range(2):
            pair[side][...] = held_ref[first : first + part, lanes[side]]
        first += part
    listed.wait()
    total = updates * count
    per = LANES // total
    group = fields // per
    tiles = group // SUBLANES
    offset = lax.axis_index("cells") * cells
    mine = lax.axis_index("cols")
    block = pl.ds(pl.multiple_of((tiles + mine // per) * LANES, LANES), LANES)

    def pick(number, carry):
        position = cells_ref[number // count, number % count] - offset

        @pl.when((position >= 0) & (position < cells))
        def _():
            lane = position % LANES
            here = pl.ds(pl.multiple_of(position - lane, LANES), LANES)

            def place(out, tile, target):
                tile = pltpu.roll(tile, (target + LANES - lane) % LANES, 1)
                at = lax.broadcasted_iota(jnp.int32, tile.shape, 1)
                small_ref[:, out] = jnp.where(at == target, tile, small_ref[:, out])

            for slot in range(per):
                for tile in range(tiles):
                    row = slot * group + tile * SUBLANES
                    out = slice(tile * LANES, (tile + 1) * LANES)
                    place(out, held_ref[row : row + SUBLANES, here], number + slot * total)
            place(block, own_ref[:, here], number + mine % per * total)

        return carry

    lax.fori_loop(0, total, pick, 0)


def invert_small(matrix):
    size = matrix.shape[0]
    row = lax.broadcasted_iota(jnp.int32, (size, size), 0)
    col = lax.broadcasted_iota(jnp.int32, (size, size), 1)
    joined = jnp.concatenate([matrix, jnp.where(row == col, 1.0, 0.0)], axis=1)
    row = lax.broadcasted_iota(jnp.int32, joined.shape, 0)
    for column in range(size):
        scaled = joined[column : column + 1, :] / joined[column : column + 1, column : column + 1]
        reduced = joined - joined[:, column : column + 1] * scaled
        joined = jnp.where(row == column, jnp.broadcast_to(scaled, joined.shape), reduced)
    return joined[:, size:]


def coefficients(order, held, picks_ref, blocks_ref, noise_ref, out_ref, joined_ref):
    updates, count = noise_ref.shape
    shards = len(order)
    padded = out_ref.shape[1] // shards
    total = updates * count
    per = LANES // total

    def slot(value, number):
        return value if number == 0 else pltpu.roll(value, LANES - number * total, 1)

    for shard in range(shards):
        first = shard // per * LANES
        rows = slot(blocks_ref[:, first : first + LANES], shard % per)
        for update in range(updates):
            at = update * count + shard * held
            joined_ref[at : at + held, :] = rows[update * held : (update + 1) * held, :]
    row = lax.broadcasted_iota(jnp.int32, (count, count), 0)
    col = lax.broadcasted_iota(jnp.int32, (count, count), 1)
    eye = jnp.where(row == col, 1.0, 0.0)

    def second(value):
        return pltpu.roll(value, LANES - count, 1)[:, :count]

    def regular(block, update):
        turned = product(block, eye, ((0,), (0,)))
        noise = jnp.broadcast_to(noise_ref[update : update + 1, :], (count, count))
        return 0.5 * (block + turned) + eye * noise

    first_rows = joined_ref[:count, :]
    cross = second(first_rows)
    inverse = invert_small(regular(first_rows[:, :count], 0))
    cross_gain = product(inverse, cross)
    revised = second(joined_ref[count:, :]) - product(cross, cross_gain, ((0,), (0,)))
    second_inverse = invert_small(regular(revised, 1))
    packed = [picks_ref[:, at : at + LANES] for at in range(0, picks_ref.shape[1], LANES)]
    picks = jnp.concatenate([slot(tile, number) for number in range(per) for tile in packed], axis=0)
    first_picks = picks[:, :count]
    second_picks = second(picks) - product(first_picks, cross_gain)
    later = product(second_picks, second_inverse)
    earlier = product(first_picks - product(later, cross, ((1,), (1,))), inverse)
    mine = lax.axis_index("cols")
    total = jnp.zeros(out_ref.shape, jnp.float32)
    source = lax.broadcasted_iota(jnp.int32, (count, out_ref.shape[1]), 0)
    target = lax.broadcasted_iota(jnp.int32, (count, out_ref.shape[1]), 1)
    for update, value in enumerate((earlier, later)):
        place = jnp.full(source.shape, -1, jnp.int32)
        for slot, other in enumerate(order):
            shard = mine ^ other
            for index in range(held):
                hit = source == shard * held + index
                place = jnp.where(hit, slot * padded + update * held + index, place)
        total = total + product(value, jnp.where(target == place, 1.0, 0.0))
    out_ref[...] = total


def split(value):
    pieces = []
    for _ in range(3):
        piece = value.astype(jnp.bfloat16)
        pieces.append(piece)
        value = value - piece.astype(jnp.float32)
    return pieces


TERMS = ((0, 0), (0, 1), (1, 0), (0, 2), (2, 0), (1, 1))


def correction(early, parts, gains_ref, *refs):
    early_refs, part_refs = refs[:early], refs[early : early + parts]
    out_ref, *held_refs = refs[early + parts : -2]
    done_ref, sems = refs[-2:]
    pieces = split(gains_ref[...])
    left = jnp.concatenate([pieces[one] for one, _ in TERMS], axis=1)
    ready = done_ref.shape[0]
    width = 512
    copies = []
    for start in range(0, out_ref.shape[1], width):
        here = slice(start, start + width)
        pieces = split(jnp.concatenate([part[:, here] for part in part_refs], axis=0))
        right = jnp.concatenate([pieces[other] for _, other in TERMS], axis=0)
        change = jnp.dot(left, right, preferred_element_type=jnp.float32)
        first = 0
        for early_ref in early_refs:
            rows = slice(first, first + early_ref.shape[0])
            done_ref[rows, here] = early_ref[:, here] - change[rows]
            first = rows.stop
        first = ready
        for held_ref in held_refs:
            rows = slice(first, first + held_ref.shape[0])
            held_ref[:, here] = -change[rows]
            first = rows.stop
        if (start + width) * STORES % out_ref.shape[1] == 0:
            share = out_ref.shape[1] // STORES
            lanes = pl.ds(start + width - share, share)
            copy = pltpu.make_async_copy(
                done_ref.at[:, lanes], out_ref.at[pl.ds(0, ready), lanes], sems.at[len(copies)]
            )
            copy.start()
            copies.append(copy)
    for copy in copies:
        copy.wait()


def sections(buffer_ref, weight_ref, finish):
    total, fields, width = buffer_ref.shape
    groups = [slice(at, at + SUBLANES) for at in range(0, fields, SUBLANES)]
    for number in range(1, SECTIONS + 1):
        below = [buffer_ref[number - 1, group] for group in groups]
        center = [buffer_ref[number, group] for group in groups]
        for row in range(number, total - number):
            above = [buffer_ref[row + 1, group] for group in groups]
            for at, group in enumerate(groups):
                value = (
                    weight_ref[0, row] * center[at]
                    + weight_ref[1, row] * above[at]
                    + weight_ref[2, row] * below[at]
                    + weight_ref[3, row] * pltpu.roll(center[at], width - 1, 1)
                    + weight_ref[4, row] * pltpu.roll(center[at], 1, 1)
                )
                if number == SECTIONS:
                    finish(row - SECTIONS, group, value)
                else:
                    buffer_ref[row, group] = value
            below, center = center, above


def fill(buffer_ref, own_ref, a_ref, b_ref):
    total, _, width = buffer_ref.shape
    rows = total - 2 * SECTIONS
    last = rows + SECTIONS
    for row in range(rows):
        buffer_ref[SECTIONS + row] = own_ref[:, row * width : (row + 1) * width]
    for ref, base in ((a_ref, jnp.where(is_even(), last, 0)), (b_ref, jnp.where(is_even(), 0, last))):
        for row in range(SECTIONS):
            buffer_ref[base + row] = ref[:, row * width : (row + 1) * width]


def forecast_cov(own_ref, a_ref, b_ref, across_ref, along_ref, spread_ref, out_ref, weight_ref, buffer_ref):
    _, width = across_ref.shape
    edge = SECTIONS * width

    def whole(number, wind_ref):
        here = slice(edge + number * width, edge + (number + 1) * width)
        a, b = a_ref[:, here], b_ref[:, here]
        low, high = jnp.where(is_even(), b, a), jnp.where(is_even(), a, b)
        return jnp.concatenate([low, wind_ref[...], high], axis=0)

    across = 0.5 * whole(0, across_ref)
    along = 0.5 * whole(1, along_ref)
    spread = whole(2, spread_ref)
    values = (
        1.0 - 4.0 * spread,
        spread - across,
        spread + across,
        spread - along,
        spread + along,
    )
    for number, value in enumerate(values):
        for row in range(value.shape[0]):
            line = jnp.broadcast_to(value[row : row + 1, :], (SUBLANES, width))
            weight_ref[number, row] = line
    fill(buffer_ref, own_ref, a_ref, b_ref)

    def finish(row, group, value):
        out_ref[group, row * width : (row + 1) * width] = value

    sections(buffer_ref, weight_ref, finish)


def forecast_early(first, slab_ref, a_ref, b_ref, weight_ref, out_ref, buffer_ref):
    _, part, width = buffer_ref.shape
    fill(buffer_ref, slab_ref.at[pl.ds(first, part), :], a_ref, b_ref)

    def finish(row, group, value):
        out_ref[group, row * width : (row + 1) * width] = value

    sections(buffer_ref, weight_ref, finish)


def forecast_late(first, slab_ref, a_ref, b_ref, weight_ref, held_ref, *refs):
    out_ref, buffer_ref, done_ref, sems = refs[-4:]
    _, part, width = buffer_ref.shape
    here = pl.ds(first, part)
    fill(buffer_ref, slab_ref.at[here, :], a_ref, b_ref)
    rows = slab_ref.shape[1] // width
    several = rows // STORES
    copies = []

    def finish(row, group, value):
        lanes = slice(row * width, (row + 1) * width)
        done_ref[group, lanes] = held_ref[group, lanes] + value
        if (row + 1) % several == 0 and group.stop == part:
            lanes = pl.ds((row + 1 - several) * width, several * width)
            copy = pltpu.make_async_copy(
                done_ref.at[:, lanes], out_ref.at[here, lanes], sems.at[len(copies)]
            )
            copy.start()
            copies.append(copy)

    sections(buffer_ref, weight_ref, finish)
    for copy in copies:
        copy.wait()


def chunk_sizes(fields):
    groups, rest = divmod(fields, SUBLANES)
    assert rest == 0 and groups >= CHUNKS
    share, rest = divmod(groups - 1, CHUNKS - 1)
    return [SUBLANES] + [(share + (at < rest)) * SUBLANES for at in range(CHUNKS - 1)]


def local(
    slab_cols, observed_cov, observed_cells, noise_variance, wind_across, wind_along, diffusion
):
    fields, cells = slab_cols.shape
    updates, held, _ = observed_cov.shape
    rows, width = wind_across.shape
    edge = SECTIONS * width
    total_rows = rows + 2 * SECTIONS
    padded = -(-updates * held // SUBLANES) * SUBLANES
    shards = lax.axis_size("cols")
    parts_of = chunk_sizes(fields)
    winds = (wind_across, wind_along, diffusion)

    assert padded == SUBLANES
    per = LANES // observed_cells.size
    picked = fields // per // SUBLANES * LANES
    small_lanes = picked + -(-shards // per) * LANES
    first_lanes = edge + 3 * width
    cov_own, *edges = pl.pallas_call(
        pack,
        out_shape=[f32(padded, cells), f32(padded, first_lanes), f32(padded, first_lanes)],
        in_specs=[HBM] * 4,
        out_specs=[VMEM] * 3,
        scratch_shapes=[
            pltpu.VMEM(observed_cov.shape, jnp.float32),
            pltpu.SemaphoreType.DMA((7,)),
        ],
        compiler_params=LIMIT,
        cost_estimate=cost(0, 8 * padded * cells),
        name="pack",
    )(*map(in_hbm, (observed_cov, *winds)))
    slab, small, *sends = pl.pallas_call(
        functools.partial(select, width),
        out_shape=[f32(fields, cells), f32(padded, small_lanes)]
        + [f32(part, edge) for part in parts_of for _ in range(2)],
        in_specs=[HBM, HBM, VMEM],
        out_specs=[VMEM] * (2 + 2 * len(parts_of)),
        scratch_shapes=[
            pltpu.SMEM(observed_cells.shape, jnp.int32),
            pltpu.SemaphoreType.DMA((1 + len(parts_of),)),
        ],
        compiler_params=LIMIT,
        cost_estimate=cost(0, 8 * fields * cells),
        name="select",
    )(in_hbm(observed_cells), in_hbm(slab_cols), cov_own)

    def exchange(pair):
        count = lax.axis_size("cells")
        assert count % 2 == 0
        a = swap(pair[0], "cells", 1)
        b = lax.ppermute(
            pair[1], "cells", [(i, (i + (1 if i % 2 else -1)) % count) for i in range(count)]
        )
        return a, b

    cov_a, cov_b = exchange(edges)
    arrived = [exchange(sends[2 * chunk : 2 * chunk + 2]) for chunk in range(len(parts_of))]
    for bit in bits_of("cells"):
        other = swap(small, "cells", bit)
        small = small + other
    picks = small[:, :picked]
    blocks = small[:, picked:]
    for bit in bits_of("cols"):
        other = swap(blocks, "cols", bit)
        blocks = blocks + other

    cov_after, weights = pl.pallas_call(
        forecast_cov,
        out_shape=(f32(padded, cells), f32(COEFFICIENTS, total_rows, SUBLANES, width)),
        in_specs=[VMEM] * 6,
        out_specs=(VMEM,) * 2,
        scratch_shapes=[pltpu.VMEM((total_rows, padded, width), jnp.float32)],
        compiler_params=LIMIT,
        cost_estimate=cost(80 * padded * cells, 16 * padded * cells),
        name="forecast_cov",
    )(cov_own, cov_a, cov_b, *winds)
    order = [0]
    parts = [cov_after]
    for bit in reversed(bits_of("cols")):
        order = order + [other ^ bit for other in order]
        for value in list(parts):
            parts.append(swap(value, "cols", bit))

    gains = pl.pallas_call(
        functools.partial(coefficients, order, held),
        out_shape=f32(fields, shards * padded),
        in_specs=[VMEM] * 3,
        out_specs=VMEM,
        scratch_shapes=[pltpu.VMEM((updates * noise_variance.shape[1], LANES), jnp.float32)],
        compiler_params=LIMIT,
        cost_estimate=cost(10**7, 10**6),
        name="coefficients",
    )(picks, blocks, noise_variance)
    first = 0
    early = []
    for chunk, part in enumerate(parts_of[:EARLY]):
        value = pl.pallas_call(
            functools.partial(forecast_early, first),
            out_shape=f32(part, cells),
            in_specs=[VMEM] * 4,
            out_specs=VMEM,
            scratch_shapes=[pltpu.VMEM((total_rows, part, width), jnp.float32)],
            compiler_params=LIMIT,
            cost_estimate=cost(120 * part * cells, 16 * part * cells),
        )(slab, *arrived[chunk], weights)
        early.append(value)
        first += part
    result, *kept = pl.pallas_call(
        functools.partial(correction, len(early), len(parts)),
        out_shape=[f32(fields, cells)] + [f32(part, cells) for part in parts_of[EARLY:]],
        in_specs=[VMEM] * (1 + len(early) + len(parts)),
        out_specs=[HBM] + [VMEM] * len(parts_of[EARLY:]),
        scratch_shapes=[
            pltpu.VMEM((first, cells), jnp.float32),
            pltpu.SemaphoreType.DMA((STORES,)),
        ],
        compiler_params=LIMIT,
        cost_estimate=cost(12 * fields * shards * padded * cells, 4 * fields * cells),
        name="correction",
    )(gains, *early, *parts)
    for chunk, part in enumerate(parts_of[EARLY:], EARLY):
        result = pl.pallas_call(
            functools.partial(forecast_late, first),
            out_shape=f32(fields, cells),
            in_specs=[VMEM] * 5 + [HBM],
            out_specs=HBM,
            scratch_shapes=[
                pltpu.VMEM((total_rows, part, width), jnp.float32),
                pltpu.VMEM((part, cells), jnp.float32),
                pltpu.SemaphoreType.DMA((STORES,)),
            ],
            input_output_aliases={5: 0},
            compiler_params=LIMIT,
            cost_estimate=cost(120 * part * cells, 16 * part * cells),
        )(slab, *arrived[chunk], weights, kept[chunk - EARLY], result)
        first += part
    return result


def solution(mesh):
    return jax.shard_map(
        local,
        mesh=mesh,
        in_specs=(
            P("cols", "cells"),
            P(None, "cols", "cells"),
            P(),
            P(),
            P("cells", None),
            P("cells", None),
            P("cells", None),
        ),
        out_specs=P("cols", "cells"),
        check_vma=False,
    )
```
